32 devices in a mesh: tm: 8 (over y, x, core), chan: 4 (over z).
Axes of the slice: x: 2, y: 2, z: 4, core: 2. Of those that a mesh axis runs over, the one named last changes fastest.
Arguments:
- volts: bfloat16 [4, 16, 12288, 256], P(None, 'chan', 'tm'), may hold values from -6 to 6
- delay_peak: int32 [128, 128], P('tm', 'chan'), may hold values from 0 to 32767
- rate_peak: int32 [128, 128], P('tm', 'chan'), may hold values from 0 to 15
- station_order: int32 [128], replicated, may hold values from 0 to 127, each once
- ref_station: int32 [1], replicated, may hold values from 0 to 63
Outputs:
- fringe: float32 [128, 128, 2, 8], P('tm', 'chan')
- normal: float32 [128, 2, 256], P('tm', None, 'chan')
- rhs: float32 [128, 2], P('tm')
The draws below stay inside these ranges and needn't reach their ends.
Inputs may be any that keep to these rules, and one draw needn't show every extreme that they name: `station_order`: each input appears once.
All inputs are finite; a program needn't handle non-finite values.
Results may differ from the reference program's by a relative error of at most 0.0003.
Values sent between devices are 32-bit elements; how exact they have to be, the bound alone decides.
A program may use at most 64 MiB of HBM per device.

```python
import math
import jax
import jax.numpy as jnp
from jax import lax

STATIONS = 64
INPUTS = 128
BAND = 16384
PERIODS_ALL = 8
NA = 4
CHANNELS = 16
SAMPLES = 12288
WD = 4
WR = 2


def place_ends(drawn, stream_key, smallest, largest):
    longest = drawn.shape.index(max(drawn.shape))
    spots = []
    for shift in (0, 1):
        where = [jax.random.randint(jax.random.fold_in(stream_key, axis), (), 0, length) for axis, length in enumerate(drawn.shape)]
        where[longest] = (where[longest] + shift) % drawn.shape[longest]
        spots.append(tuple(where))
    return drawn.at[spots[0]].set(smallest).at[spots[1]].set(largest)


def shard_levels(stream_key, dims, pieces, smallest, high):
    factor_of, own = 1.0, jax.random.fold_in(stream_key, 6)
    for dim, blocks in pieces:
        heights = jnp.exp(jax.random.uniform(jax.random.fold_in(own, dim), (blocks,), jnp.float32, smallest / len(pieces), high / len(pieces)))
        factor_of = factor_of * jnp.repeat(heights, dims[dim] // blocks).reshape([-1 if axis == dim else 1 for axis in range(len(dims))])
    return factor_of


def centred(rng, shape, scale, reach, pieces=(), held_as=jnp.bfloat16):
    result = jax.random.normal(rng, shape, jnp.float32) * scale
    if len(pieces) > 0:
        result = shard_levels(rng, shape, pieces, -0.22, 0.18) * result
    return jnp.clip(result, min=-reach, max=reach).astype(held_as)


def setup_inputs(seed: int = 0) -> dict:
    splits = jax.random.split(jax.random.key(seed), 6)
    volts = centred(splits[0], (NA, CHANNELS, SAMPLES, 2 * INPUTS), 1.0, 6.0, ((1, 4), (2, 8)))
    delay_peak = place_ends(jax.random.randint(splits[1], (INPUTS, INPUTS), 0, 2 * BAND), jax.random.fold_in(splits[1], 1), 0, (2 * BAND) - 1).astype(jnp.int32)
    rate_peak = place_ends(jax.random.randint(splits[2], (INPUTS, INPUTS), 0, 2 * PERIODS_ALL), jax.random.fold_in(splits[2], 1), 0, (2 * PERIODS_ALL) - 1).astype(jnp.int32)
    station_order = jax.random.permutation(splits[3], INPUTS).astype(jnp.int32)
    ref_station = jax.random.randint(splits[4], (1,), 0, STATIONS).astype(jnp.int32)
    return dict(volts=volts, delay_peak=delay_peak, rate_peak=rate_peak, station_order=station_order, ref_station=ref_station)


def fringe_window(vis_re, vis_im, dpeak, rpeak, chan_start, chans_total, periods):
    chan_local = vis_re.shape[3]
    dgrid = 2 * BAND
    rgrid = 2 * PERIODS_ALL
    dstep = BAND // chans_total
    rstep = PERIODS_ALL // periods
    chan_idx = chan_start + jnp.arange(chan_local, dtype=jnp.int32)
    period_idx = jnp.arange(periods, dtype=jnp.int32)
    delays = dpeak[:, :, None] + (jnp.arange(WD, dtype=jnp.int32) - WD // 2) * dstep
    rates = rpeak[:, :, None] + (jnp.arange(WR, dtype=jnp.int32) - WR // 2) * rstep
    dphase = jnp.mod(delays[..., None] * chan_idx, dgrid).astype(jnp.float32) * (2.0 * math.pi / dgrid)
    rphase = jnp.mod(rates[..., None] * period_idx, rgrid).astype(jnp.float32) * (2.0 * math.pi / rgrid)
    angle = rphase[:, :, :, None, :, None] + dphase[:, :, None, :, None, :]
    cosine = jnp.cos(angle)
    sine = jnp.sin(angle)
    vr = vis_re[:, :, None, None]
    vi = vis_im[:, :, None, None]
    fre = jnp.sum(vr * cosine + vi * sine, axis=(4, 5))
    fim = jnp.sum(vi * cosine - vr * sine, axis=(4, 5))
    return fre, fim


def normal_terms(fre, fim, row_inputs, col_inputs, inputs):
    power = fre * fre + fim * fim
    udel = (2.0 * jnp.arange(WD, dtype=jnp.float32) + 1.0 - WD) / WD
    urat = (2.0 * jnp.arange(WR, dtype=jnp.float32) + 1.0 - WR) / WR
    udel = udel[None, :]
    urat = urat[:, None]
    m_dd = jnp.mean(power * udel * udel, axis=(2, 3))
    m_dr = jnp.mean(power * udel * urat, axis=(2, 3))
    m_rr = jnp.mean(power * urat * urat, axis=(2, 3))
    g_d = jnp.mean(power * udel, axis=(2, 3))
    g_r = jnp.mean(power * urat, axis=(2, 3))
    slots = jnp.arange(inputs, dtype=jnp.int32)
    incidence = (row_inputs[:, None, None] == slots).astype(jnp.float32) - (col_inputs[None, :, None] == slots).astype(jnp.float32)
    flat = incidence.reshape(-1, inputs)

    def block(weight):
        scaled = (incidence * weight[:, :, None]).reshape(-1, inputs)
        return jnp.dot(scaled.T, flat, precision=lax.Precision.HIGHEST) / inputs

    n_dd = block(m_dd)
    n_dr = block(m_dr)
    n_rr = block(m_rr)
    normal = jnp.concatenate([jnp.concatenate([n_dd, n_dr], 1), jnp.concatenate([n_dr, n_rr], 1)], 0)
    rhs_d = jnp.dot(g_d.reshape(-1), flat, precision=lax.Precision.HIGHEST) / inputs
    rhs_r = jnp.dot(g_r.reshape(-1), flat, precision=lax.Precision.HIGHEST) / inputs
    return normal, jnp.concatenate([rhs_d, rhs_r])


def reference(volts, delay_peak, rate_peak, station_order, ref_station):
    periods, chans, samples, width = volts.shape
    inputs = width // 2
    scale = float(samples) ** -0.5

    def cross(block_volts):
        prod = jnp.dot(block_volts.T, block_volts, preferred_element_type=jnp.float32)
        real = prod[:inputs, :inputs] + prod[inputs:, inputs:]
        imag = prod[:inputs, inputs:] - prod[inputs:, :inputs]
        return jnp.stack([real, imag]) * scale

    vis = lax.map(cross, volts.reshape(periods * chans, samples, width))
    vis = vis.reshape(periods, chans, 2, inputs, inputs)
    grouped = jnp.take(vis, station_order, axis=4)
    vis_re = jnp.transpose(grouped[:, :, 0], (2, 3, 0, 1))
    vis_im = jnp.transpose(grouped[:, :, 1], (2, 3, 0, 1))
    fre, fim = fringe_window(vis_re, vis_im, delay_peak, rate_peak, 0, chans, periods)
    spread = float(periods * chans) ** -0.5
    row_inputs = jnp.arange(inputs, dtype=jnp.int32)
    auto = row_inputs[:, None] == station_order[None, :]
    fre = jnp.where(auto[:, :, None, None], 0.0, fre * spread)
    fim = jnp.where(auto[:, :, None, None], 0.0, fim * spread)
    fringe = jnp.stack([fre, fim], axis=2).reshape(inputs, inputs, 2, WR * WD)
    normal, rhs = normal_terms(fre, fim, row_inputs, station_order, inputs)
    params = jnp.arange(2 * inputs, dtype=jnp.int32)
    isref = (params % inputs) // 2 == ref_station[0]
    ident = (params[:, None] == params[None, :]).astype(jnp.float32)
    normal = jnp.where(isref[:, None] | isref[None, :], ident, normal)
    rhs = jnp.where(isref, 0.0, rhs)
    normal = jnp.transpose(normal.reshape(2, inputs, 2 * inputs), (1, 0, 2))
    rhs = jnp.transpose(rhs.reshape(2, inputs), (1, 0))
    return fringe, normal, rhs
```

```python
import functools
import math

import jax
import jax.numpy as jnp
from jax import lax
from jax.experimental import pallas as pl
from jax.experimental.pallas import tpu as pltpu
from jax.sharding import PartitionSpec as P

BAND = 16384
PERIODS_ALL = 8
WD = 4
WR = 2


def fringe_window(vis_re, vis_im, dpeak, rpeak, chans_total, periods):
    chan_local = vis_re.shape[3]
    dgrid = 2 * BAND
    rgrid = 2 * PERIODS_ALL
    dstep = BAND // chans_total
    rstep = PERIODS_ALL // periods
    chan_idx = jnp.arange(chan_local, dtype=jnp.int32)
    period_idx = jnp.arange(periods, dtype=jnp.int32)
    delays = dpeak[:, :, None] + (jnp.arange(WD, dtype=jnp.int32) - WD // 2) * dstep
    rates = rpeak[:, :, None] + (jnp.arange(WR, dtype=jnp.int32) - WR // 2) * rstep
    dphase = jnp.mod(delays[..., None] * chan_idx, dgrid).astype(jnp.float32) * (
        2.0 * math.pi / dgrid
    )
    rphase = jnp.mod(rates[..., None] * period_idx, rgrid).astype(jnp.float32) * (
        2.0 * math.pi / rgrid
    )
    angle = rphase[:, :, :, None, :, None] + dphase[:, :, None, :, None, :]
    cosine = jnp.cos(angle)
    sine = jnp.sin(angle)
    vr = vis_re[:, :, None, None]
    vi = vis_im[:, :, None, None]
    fre = jnp.sum(vr * cosine + vi * sine, axis=(4, 5))
    fim = jnp.sum(vi * cosine - vr * sine, axis=(4, 5))
    return (fre, fim)


def baseline_weights(fre, fim):
    power = fre * fre + fim * fim
    udel = (2.0 * jnp.arange(WD, dtype=jnp.float32) + 1.0 - WD) / WD
    urat = (2.0 * jnp.arange(WR, dtype=jnp.float32) + 1.0 - WR) / WR
    udel = udel[None, :]
    urat = urat[:, None]
    m_dd = jnp.mean(power * udel * udel, axis=(2, 3))
    m_dr = jnp.mean(power * udel * urat, axis=(2, 3))
    m_rr = jnp.mean(power * urat * urat, axis=(2, 3))
    g_d = jnp.mean(power * udel, axis=(2, 3))
    g_r = jnp.mean(power * urat, axis=(2, 3))
    return jnp.stack([m_dd, m_dr, m_rr, g_d, g_r])


def normal_terms(weights, row_inputs, col_inputs, inputs):
    slots = jnp.arange(inputs, dtype=jnp.int32)
    incidence = (row_inputs[:, None, None] == slots).astype(jnp.float32) - (
        col_inputs[None, :, None] == slots
    ).astype(jnp.float32)
    flat = incidence.reshape(-1, inputs)

    def block(weight):
        scaled = (incidence * weight[:, :, None]).reshape(-1, inputs)
        return jnp.dot(scaled.T, flat, precision=lax.Precision.HIGHEST) / inputs

    n_dd = block(weights[0])
    n_dr = block(weights[1])
    n_rr = block(weights[2])
    normal = jnp.concatenate(
        [jnp.concatenate([n_dd, n_dr], 1), jnp.concatenate([n_dr, n_rr], 1)], 0
    )
    rhs_d = jnp.dot(weights[3].reshape(-1), flat, precision=lax.Precision.HIGHEST) / inputs
    rhs_r = jnp.dot(weights[4].reshape(-1), flat, precision=lax.Precision.HIGHEST) / inputs
    return (normal, jnp.concatenate([rhs_d, rhs_r]))


def full_gram(volts, inputs, scale):
    prod = jnp.einsum("acti,actj->iacj", volts, volts, preferred_element_type=jnp.float32)
    real = prod[:inputs, :, :, :inputs] + prod[inputs:, :, :, inputs:]
    imag = prod[:inputs, :, :, inputs:] - prod[inputs:, :, :, :inputs]
    return jnp.stack([real, imag], axis=3) * scale


def body(volts, delay_peak, rate_peak, station_order, ref_station):
    periods, chans, samples, width = volts.shape
    inputs = width // 2
    row_count = delay_peak.shape[0]
    col_count = delay_peak.shape[1]
    time_devs = lax.axis_size("tm")
    chan_devs = lax.axis_size("chan")
    chans_total = chans * chan_devs
    scale = float(samples * time_devs) ** (-0.5)
    spread = float(periods * chans_total) ** (-0.5)
    col_inputs = lax.dynamic_slice_in_dim(
        station_order, lax.axis_index("chan") * col_count, col_count
    )
    row_inputs = lax.axis_index("tm") * row_count + jnp.arange(row_count, dtype=jnp.int32)
    gram = full_gram(volts, inputs, scale)
    summed = lax.psum_scatter(
        gram.reshape(lax.axis_size("tm") * row_count, -1), "tm", scatter_dimension=0, tiled=True
    )
    vis = summed.reshape(row_count, periods, chans, 2, inputs)
    grouped = jnp.take(vis, station_order, axis=4)
    moved = lax.all_to_all(grouped, "chan", split_axis=4, concat_axis=2, tiled=True)
    vis_re = jnp.transpose(moved[:, :, :, 0], (0, 3, 1, 2))
    vis_im = jnp.transpose(moved[:, :, :, 1], (0, 3, 1, 2))
    fre, fim = fringe_window(vis_re, vis_im, delay_peak, rate_peak, chans_total, periods)
    auto = (row_inputs[:, None] == col_inputs[None, :])[:, :, None, None]
    fre = jnp.where(auto, 0.0, fre * spread)
    fim = jnp.where(auto, 0.0, fim * spread)
    fringe = jnp.stack([fre, fim], axis=2).reshape(row_count, col_count, 2, WR * WD)
    weights = baseline_weights(fre, fim)
    col_width = 2 * inputs // chan_devs
    normal_part, rhs_part = normal_terms(weights, row_inputs, col_inputs, inputs)
    arranged = jnp.transpose(normal_part.reshape(2, inputs, 2 * inputs), (1, 0, 2))
    arranged = arranged.reshape(time_devs, row_count, 2, chan_devs, col_width)
    arranged = jnp.transpose(arranged, (0, 3, 1, 2, 4)).reshape(
        time_devs * chan_devs * row_count, 2, col_width
    )
    normal_rows = lax.psum_scatter(arranged, ("tm", "chan"), scatter_dimension=0, tiled=True)
    rhs_all = lax.psum(jnp.transpose(rhs_part.reshape(2, inputs), (1, 0)), ("tm", "chan"))
    rhs_rows = lax.dynamic_slice_in_dim(rhs_all, lax.axis_index("tm") * row_count, row_count, 0)
    columns = lax.axis_index("chan") * col_width + jnp.arange(col_width, dtype=jnp.int32)
    params = jnp.arange(2, dtype=jnp.int32)[None, :] * inputs + row_inputs[:, None]
    row_ref = row_inputs // 2 == ref_station[0]
    col_ref = columns % inputs // 2 == ref_station[0]
    ident = (params[:, :, None] == columns[None, None, :]).astype(jnp.float32)
    normal_rows = jnp.where(row_ref[:, None, None] | col_ref[None, None, :], ident, normal_rows)
    rhs_rows = jnp.where(row_ref[:, None], 0.0, rhs_rows)
    return (fringe, normal_rows, rhs_rows)


TM = 8
MESH = pl.DeviceIdType.MESH
TURN = 2 * BAND


def unit(steps):
    quarter = TURN // 4
    quad = lax.shift_right_logical(steps + quarter // 2, quarter.bit_length() - 1)
    x = (steps - quad * quarter).astype(jnp.float32) * (2.0 * math.pi / TURN)
    y = x * x
    s = x * (1.0 + y * (-1.0 / 6 + y * (1.0 / 120 + y * (-1.0 / 5040 + y * (1.0 / 362880)))))
    c = 1.0 + y * (-0.5 + y * (1.0 / 24 + y * (-1.0 / 720 + y * (1.0 / 40320 + y * (-1.0 / 3628800)))))
    odd = (quad & 1) == 1
    cosine = jnp.where(odd, s, c)
    sine = jnp.where(odd, c, s)
    cosine = jnp.where(((quad + 1) & 2) == 2, -cosine, cosine)
    sine = jnp.where((quad & 2) == 2, -sine, sine)
    return cosine, sine


def cmul(a, b):
    return a[0] * b[0] - a[1] * b[1], a[0] * b[1] + a[1] * b[0]


def cadd(a, b):
    return b if a is None else (a[0] + b[0], a[1] + b[1])


def cconst(a, turns):
    turns = turns % 1.0
    if turns == 0.0:
        return a
    if turns == 0.25:
        return a[1], -a[0]
    if turns == 0.5:
        return -a[0], -a[1]
    if turns == 0.75:
        return -a[1], a[0]
    c, s = math.cos(2 * math.pi * turns), math.sin(2 * math.pi * turns)
    return a[0] * c + a[1] * s, a[1] * c - a[0] * s


def fused(
    nchan, volts, dpk, rpk, order, ref, fringe_out, normal_out, rhs_out,
    xbuf, vre, vim, pkl, pka, pkb, part, sbuf, rb1, rb2, zs, rz, wz, nat, rx,
    vsem, asend, arecv, bsend, brecv, s1, r1, s2, r2, s3, r3, s4, r4, s5, r5,
):
    i, j = lax.axis_index("tm"), lax.axis_index("chan")
    periods, chans, samples, width = volts.shape
    inputs = width // 2
    rows, cols = dpk.shape
    chans_total = chans * nchan
    core, cx, cy = i % 2, (i // 2) % 2, i // 4
    sibling = i + 1 - 2 * core
    scale = float(samples * TM) ** (-0.5) * float(periods * chans_total) ** (-0.5)

    def chip(r, c):
        return ((((cy + r // 2) % 2) * 2) + (cx + r % 2) % 2) * 2 + c

    def load(n):
        return pltpu.make_async_copy(volts.at[n // chans, n % chans], xbuf.at[n], vsem.at[n])

    def remote(src, dst, ssem, rsem, to_i, to_j):
        return pltpu.make_async_remote_copy(
            src_ref=src, dst_ref=dst, send_sem=ssem, recv_sem=rsem,
            device_id=(to_i, to_j), device_id_type=MESH,
        )

    @pl.loop(0, periods * chans)
    def _(n):
        load(n).start()

    pkl[...] = jnp.zeros_like(pkl)
    pkl[:, 0:cols] = dpk[...]
    pkl[:, cols : 2 * cols] = rpk[...]

    barrier = pltpu.get_barrier_semaphore()
    for d in range(1, TM):
        pl.semaphore_signal(barrier, inc=1, device_id=((i + d) % TM, j), device_id_type=MESH)
    for d in range(1, nchan):
        pl.semaphore_signal(barrier, inc=1, device_id=(i, (j + d) % nchan), device_id_type=MESH)
    pl.semaphore_wait(barrier, TM - 1 + nchan - 1)

    acopies = [
        remote(pkl, pka.at[d - 1], asend.at[d - 1], arecv.at[d - 1], i, (j + d) % nchan)
        for d in range(1, nchan)
    ]
    for copy in acopies:
        copy.start()

    def gram(n):
        load(n).wait()
        x = xbuf[n]
        g = lax.dot_general(x, x, (((0,), (0,)), ((), ())), preferred_element_type=jnp.float32)
        vre[n] = g[:inputs, :inputs] + g[inputs:, inputs:]
        vim[n] = g[:inputs, inputs:] - g[inputs:, :inputs]

    @pl.loop(0, 4)
    def _(n):
        gram(n)

    hot = (
        lax.broadcasted_iota(jnp.int32, (inputs, inputs), 0)
        == jnp.broadcast_to(order[...], (inputs, inputs))
    ).astype(jnp.float32)
    hot_t = hot.T

    for copy in acopies:
        copy.wait()
    blocks = [pkl[...]] + [pka[d] for d in range(nchan - 1)]
    ordered = []
    for g in range(nchan):
        pick = blocks[0]
        for d in range(1, nchan):
            pick = jnp.where((j + nchan - d) % nchan == g, blocks[d], pick)
        ordered.append(pick)
    dall = jnp.concatenate([b[:, 0:cols] for b in ordered], axis=1)
    rall = jnp.concatenate([b[:, cols : 2 * cols] for b in ordered], axis=1)
    digits = jnp.concatenate(
        [
            lax.shift_right_logical(dall, 8).astype(jnp.float32),
            (dall & 255).astype(jnp.float32),
            rall.astype(jnp.float32),
        ],
        axis=0,
    )
    moved = jnp.dot(
        digits.astype(jnp.bfloat16), hot_t.astype(jnp.bfloat16), preferred_element_type=jnp.float32
    )
    pkb[i, 0] = (moved[0:rows] * 256.0 + moved[rows : 2 * rows]).astype(jnp.int32)
    pkb[i, 1] = moved[2 * rows : 3 * rows].astype(jnp.int32)
    bcopies = [
        remote(pkb.at[i], pkb.at[i], bsend.at[d - 1], brecv.at[d - 1], (i + d) % TM, j)
        for d in range(1, TM)
    ]
    for copy in bcopies:
        copy.start()

    @pl.loop(4, periods * chans)
    def _(n):
        gram(n)

    for copy in bcopies:
        copy.wait()

    def by_chan(values):
        pick = jnp.float32(values[0])
        for g in range(1, nchan):
            pick = jnp.where(j == g, jnp.float32(values[g]), pick)
        return pick

    dturn = (BAND // chans_total) / TURN
    rturn = (PERIODS_ALL // periods) / (2 * PERIODS_ALL)
    shifts = []
    for wd in range(WD):
        angles = [2 * math.pi * (wd - WD // 2) * g * chans * dturn for g in range(nchan)]
        shifts.append(
            (by_chan([math.cos(t) for t in angles]), by_chan([-math.sin(t) for t in angles]))
        )

    def window(ip, h):
        at = pl.ds(pl.multiple_of(ip * rows + h * 8, 8), 8)
        dl = pkb[ip, 0, h * 8 : h * 8 + 8, :]
        rl = pkb[ip, 1, h * 8 : h * 8 + 8, :]
        c, s = unit(dl)
        z1 = (c, -s)
        c, s = unit((dl * (j * chans)) & (TURN - 1))
        ed = (c, -s)
        c, s = unit(rl * (BAND // PERIODS_ALL))
        er = [None, (c, -s)]
        for a in range(2, periods):
            er.append(cmul(er[-1], er[1]))
        acc = [None] * (WR * WD)
        for l in range(chans):
            us = [None] * WR
            for a in range(periods):
                v = (vre[a * chans + l, at, :], vim[a * chans + l, at, :])
                if a:
                    v = cmul(v, er[a])
                for wr in range(WR):
                    us[wr] = cadd(us[wr], cconst(v, (wr - WR // 2) * a * rturn))
            if l:
                ed = cmul(ed, z1)
            for wr in range(WR):
                u = cmul(us[wr], ed)
                for wd in range(WD):
                    term = cconst(u, (wd - WD // 2) * l * dturn)
                    acc[wr * WD + wd] = cadd(acc[wr * WD + wd], term)
        out = []
        for w in range(WR * WD):
            wd = w % WD
            out.append(acc[w] if wd == WD // 2 else cmul(acc[w], shifts[wd]))
        return [o[0] for o in out] + [o[1] for o in out]

    @pl.loop(0, 8)
    def _(u):
        r = 3 - u % 4
        first = u < 4
        side = jnp.where(first, 1 - core, core)
        ip = chip(r, side)
        for h in range(rows // 8):
            values = window(ip, h)
            for v, value in enumerate(values):
                part[u, v, h * 8 : h * 8 + 8, :] = value

        @pl.when(first)
        def _():
            remote(part.at[u], rb1.at[r], s1.at[r], r1.at[r], sibling, j).start()

        @pl.when(u >= 4)
        def _():
            remote(part.at[3 - r], rb1.at[r], s1.at[r], r1.at[r], sibling, j).wait()
            sbuf[r] = part[u] + rb1[r]

            @pl.when(r > 0)
            def _():
                remote(sbuf.at[r], rb2.at[r - 1], s2.at[r - 1], r2.at[r - 1], chip(r, core), j).start()

    bins = WR * WD
    row = lax.broadcasted_iota(jnp.int32, (bins * rows, inputs), 0)
    col = lax.broadcasted_iota(jnp.int32, (bins * rows, inputs), 1)
    w_row, kind = row // rows, col // rows
    ud = (2 * (w_row % WD) + 1 - WD).astype(jnp.float32) / WD
    ur = (2 * (w_row // WD) + 1 - WR).astype(jnp.float32) / WR
    coef = jnp.where(kind == 0, ud * ud, 0.0)
    coef = jnp.where(kind == 1, ud * ur, coef)
    coef = jnp.where(kind == 2, ur * ur, coef)
    coef = jnp.where(kind == 3, ud, coef)
    coef = jnp.where(kind == 4, ur, coef)
    coef = jnp.where(row % rows == col % rows, coef, 0.0) * (1.0 / bins)

    for r in (1, 2, 3):
        remote(sbuf.at[r], rb2.at[r - 1], s2.at[r - 1], r2.at[r - 1], chip(r, core), j).wait()
    total = (sbuf[0] + rb2[0]) + (rb2[1] + rb2[2])
    shape3 = (2 * bins, rows, inputs)
    auto = lax.broadcasted_iota(jnp.int32, shape3, 2) == (
        lax.broadcasted_iota(jnp.int32, shape3, 1) + i * rows
    )
    total = jnp.where(auto, 0.0, total * scale).reshape(2 * bins * rows, inputs)
    zs[...] = lax.dot_general(
        hot_t, total, (((1,), (1,)), ((), ())),
        precision=lax.Precision.HIGHEST, preferred_element_type=jnp.float32,
    )

    def group(g):
        return pl.ds(pl.multiple_of(g * cols, cols), cols)

    copies = []
    for d in range(1, nchan):
        to = (j + d) % nchan
        copies.append(remote(zs.at[group(to)], rz.at[d - 1], s3.at[d - 1], r3.at[d - 1], i, to))
        copies[-1].start()
    mine = zs[group(j), :]
    for d, copy in enumerate(copies):
        copy.wait()
        mine = mine + rz[d]
    fringe_out[...] = mine
    fre, fim = mine[:, : bins * rows], mine[:, bins * rows :]
    power = fre * fre + fim * fim
    wz[group(j), :] = jnp.dot(
        power, coef, precision=lax.Precision.HIGHEST, preferred_element_type=jnp.float32
    )
    copies = []
    for d in range(1, nchan):
        to = (j + d) % nchan
        copies.append(remote(wz.at[group(j)], wz.at[group(j)], s4.at[d - 1], r4.at[d - 1], i, to))
        copies[-1].start()
    for copy in copies:
        copy.wait()
    natural = jnp.dot(
        hot, wz[...], precision=lax.Precision.HIGHEST, preferred_element_type=jnp.float32
    )
    nat[...] = natural

    def rowsof(g):
        return pl.ds(pl.multiple_of(g * rows, rows), rows)

    copies = []
    for d in range(1, TM):
        to = (i + d) % TM
        copies.append(remote(nat.at[rowsof(to)], rx.at[i], s5.at[d - 1], r5.at[d - 1], to, j))
        copies[-1].start()
    rx[i] = nat[rowsof(i), :]
    straight = natural.T
    for copy in copies:
        copy.wait()
    across = [
        jnp.concatenate([rx[g, :, m * rows : (m + 1) * rows] for g in range(TM)], axis=1)
        for m in range(5)
    ]
    straight = [straight[m * rows : (m + 1) * rows] for m in range(5)]
    row_in = lax.broadcasted_iota(jnp.int32, (rows, inputs), 0) + i * rows
    col_in = lax.broadcasted_iota(jnp.int32, (rows, inputs), 1)
    diag = row_in == col_in
    isref = (lax.shift_right_logical(row_in, 1) == ref[0]) | (
        lax.shift_right_logical(col_in, 1) == ref[0]
    )
    blocks = []
    for m in range(3):
        both = straight[m] + across[m]
        sums = jnp.sum(both, axis=1, keepdims=True)
        blocks.append((jnp.where(diag, sums, 0.0) - both) * (1.0 / inputs))
    t = j * 2 // nchan
    per = nchan // 2
    span = 2 * inputs // nchan
    for s in range(2):
        block = jnp.where(t == 0, blocks[s], blocks[s + 1])
        ident = jnp.where(diag & (t == s), 1.0, 0.0)
        block = jnp.where(isref, ident, block)
        out = block[:, 0:span]
        for q in range(1, per):
            out = jnp.where(j % per == q, block[:, q * span : (q + 1) * span], out)
        normal_out[:, s, :] = out
    row_ref = lax.shift_right_logical(
        lax.broadcasted_iota(jnp.int32, (rows, 1), 0) + i * rows, 1
    ) == ref[0]
    for s in range(2):
        value = jnp.sum(straight[3 + s] - across[3 + s], axis=1, keepdims=True) * (1.0 / inputs)
        rhs_out[:, s : s + 1] = jnp.where(row_ref, 0.0, value)


def fused_body(nchan, volts, delay_peak, rate_peak, station_order, ref_station):
    periods, chans, samples, width = volts.shape
    inputs = width // 2
    rows, cols = delay_peak.shape
    bins = WR * WD
    steps = periods * chans
    f32 = jnp.float32
    vmem = pl.BlockSpec(memory_space=pltpu.VMEM)
    dma = pltpu.SemaphoreType.DMA
    fringe, normal, rhs = pl.pallas_call(
        functools.partial(fused, nchan),
        out_shape=(
            jax.ShapeDtypeStruct((cols, 2 * bins * rows), f32),
            jax.ShapeDtypeStruct((rows, 2, 2 * inputs // nchan), f32),
            jax.ShapeDtypeStruct((rows, 2), f32),
        ),
        in_specs=[
            pl.BlockSpec(memory_space=pl.ANY), vmem, vmem, vmem,
            pl.BlockSpec(memory_space=pltpu.SMEM),
        ],
        out_specs=(vmem, vmem, vmem),
        scratch_shapes=[
            pltpu.VMEM((steps, samples, width), volts.dtype),
            pltpu.VMEM((steps, inputs, inputs), f32),
            pltpu.VMEM((steps, inputs, inputs), f32),
            pltpu.VMEM((rows, inputs), jnp.int32),
            pltpu.VMEM((nchan - 1, rows, inputs), jnp.int32),
            pltpu.VMEM((TM, 2, rows, inputs), jnp.int32),
            pltpu.VMEM((TM, 2 * bins, rows, inputs), f32),
            pltpu.VMEM((4, 2 * bins, rows, inputs), f32),
            pltpu.VMEM((4, 2 * bins, rows, inputs), f32),
            pltpu.VMEM((3, 2 * bins, rows, inputs), f32),
            pltpu.VMEM((inputs, 2 * bins * rows), f32),
            pltpu.VMEM((nchan - 1, cols, 2 * bins * rows), f32),
            pltpu.VMEM((inputs, inputs), f32),
            pltpu.VMEM((inputs, inputs), f32),
            pltpu.VMEM((TM, rows, inputs), f32),
            dma((steps,)),
            dma((nchan - 1,)), dma((nchan - 1,)),
            dma((TM - 1,)), dma((TM - 1,)),
            dma((4,)), dma((4,)),
            dma((3,)), dma((3,)),
            dma((nchan - 1,)), dma((nchan - 1,)),
            dma((nchan - 1,)), dma((nchan - 1,)),
            dma((TM - 1,)), dma((TM - 1,)),
        ],
        compiler_params=pltpu.CompilerParams(
            collective_id=0, has_side_effects=True, vmem_limit_bytes=48 * 1024 * 1024
        ),
        name="fringe_fit",
    )(volts, delay_peak, rate_peak, station_order.reshape(1, inputs), ref_station)
    fringe = jnp.transpose(fringe.reshape(cols, 2, bins, rows), (3, 0, 1, 2))
    return fringe, normal, rhs


def solution(mesh):
    in_specs = (P(None, "chan", "tm", None), P("tm", "chan"), P("tm", "chan"), P(), P())
    out_specs = (P("tm", "chan", None, None), P("tm", None, "chan"), P("tm", None))
    nchan = mesh.shape["chan"]
    fits = mesh.shape["tm"] == TM and nchan == 4
    whole = functools.partial(fused_body, nchan) if fits else body
    return jax.shard_map(whole, mesh=mesh, in_specs=in_specs, out_specs=out_specs, check_vma=False)
```

```python
import functools
import math

import jax
import jax.numpy as jnp
from jax import lax
from jax.experimental import pallas as pl
from jax.experimental.pallas import tpu as pltpu
from jax.sharding import PartitionSpec as P

BAND = 16384
PERIODS_ALL = 8
WD = 4
WR = 2


def fringe_window(vis_re, vis_im, dpeak, rpeak, chans_total, periods):
    chan_local = vis_re.shape[3]
    dgrid = 2 * BAND
    rgrid = 2 * PERIODS_ALL
    dstep = BAND // chans_total
    rstep = PERIODS_ALL // periods
    chan_idx = jnp.arange(chan_local, dtype=jnp.int32)
    period_idx = jnp.arange(periods, dtype=jnp.int32)
    delays = dpeak[:, :, None] + (jnp.arange(WD, dtype=jnp.int32) - WD // 2) * dstep
    rates = rpeak[:, :, None] + (jnp.arange(WR, dtype=jnp.int32) - WR // 2) * rstep
    dphase = jnp.mod(delays[..., None] * chan_idx, dgrid).astype(jnp.float32) * (
        2.0 * math.pi / dgrid
    )
    rphase = jnp.mod(rates[..., None] * period_idx, rgrid).astype(jnp.float32) * (
        2.0 * math.pi / rgrid
    )
    angle = rphase[:, :, :, None, :, None] + dphase[:, :, None, :, None, :]
    cosine = jnp.cos(angle)
    sine = jnp.sin(angle)
    vr = vis_re[:, :, None, None]
    vi = vis_im[:, :, None, None]
    fre = jnp.sum(vr * cosine + vi * sine, axis=(4, 5))
    fim = jnp.sum(vi * cosine - vr * sine, axis=(4, 5))
    return (fre, fim)


def baseline_weights(fre, fim):
    power = fre * fre + fim * fim
    udel = (2.0 * jnp.arange(WD, dtype=jnp.float32) + 1.0 - WD) / WD
    urat = (2.0 * jnp.arange(WR, dtype=jnp.float32) + 1.0 - WR) / WR
    udel = udel[None, :]
    urat = urat[:, None]
    m_dd = jnp.mean(power * udel * udel, axis=(2, 3))
    m_dr = jnp.mean(power * udel * urat, axis=(2, 3))
    m_rr = jnp.mean(power * urat * urat, axis=(2, 3))
    g_d = jnp.mean(power * udel, axis=(2, 3))
    g_r = jnp.mean(power * urat, axis=(2, 3))
    return jnp.stack([m_dd, m_dr, m_rr, g_d, g_r])


def normal_terms(weights, row_inputs, col_inputs, inputs):
    slots = jnp.arange(inputs, dtype=jnp.int32)
    incidence = (row_inputs[:, None, None] == slots).astype(jnp.float32) - (
        col_inputs[None, :, None] == slots
    ).astype(jnp.float32)
    flat = incidence.reshape(-1, inputs)

    def block(weight):
        scaled = (incidence * weight[:, :, None]).reshape(-1, inputs)
        return jnp.dot(scaled.T, flat, precision=lax.Precision.HIGHEST) / inputs

    n_dd = block(weights[0])
    n_dr = block(weights[1])
    n_rr = block(weights[2])
    normal = jnp.concatenate(
        [jnp.concatenate([n_dd, n_dr], 1), jnp.concatenate([n_dr, n_rr], 1)], 0
    )
    rhs_d = jnp.dot(weights[3].reshape(-1), flat, precision=lax.Precision.HIGHEST) / inputs
    rhs_r = jnp.dot(weights[4].reshape(-1), flat, precision=lax.Precision.HIGHEST) / inputs
    return (normal, jnp.concatenate([rhs_d, rhs_r]))


def full_gram(volts, inputs, scale):
    prod = jnp.einsum("acti,actj->iacj", volts, volts, preferred_element_type=jnp.float32)
    real = prod[:inputs, :, :, :inputs] + prod[inputs:, :, :, inputs:]
    imag = prod[:inputs, :, :, inputs:] - prod[inputs:, :, :, :inputs]
    return jnp.stack([real, imag], axis=3) * scale


def body(volts, delay_peak, rate_peak, station_order, ref_station):
    periods, chans, samples, width = volts.shape
    inputs = width // 2
    row_count = delay_peak.shape[0]
    col_count = delay_peak.shape[1]
    time_devs = lax.axis_size("tm")
    chan_devs = lax.axis_size("chan")
    chans_total = chans * chan_devs
    scale = float(samples * time_devs) ** (-0.5)
    spread = float(periods * chans_total) ** (-0.5)
    col_inputs = lax.dynamic_slice_in_dim(
        station_order, lax.axis_index("chan") * col_count, col_count
    )
    row_inputs = lax.axis_index("tm") * row_count + jnp.arange(row_count, dtype=jnp.int32)
    gram = full_gram(volts, inputs, scale)
    summed = lax.psum_scatter(
        gram.reshape(lax.axis_size("tm") * row_count, -1), "tm", scatter_dimension=0, tiled=True
    )
    vis = summed.reshape(row_count, periods, chans, 2, inputs)
    grouped = jnp.take(vis, station_order, axis=4)
    moved = lax.all_to_all(grouped, "chan", split_axis=4, concat_axis=2, tiled=True)
    vis_re = jnp.transpose(moved[:, :, :, 0], (0, 3, 1, 2))
    vis_im = jnp.transpose(moved[:, :, :, 1], (0, 3, 1, 2))
    fre, fim = fringe_window(vis_re, vis_im, delay_peak, rate_peak, chans_total, periods)
    auto = (row_inputs[:, None] == col_inputs[None, :])[:, :, None, None]
    fre = jnp.where(auto, 0.0, fre * spread)
    fim = jnp.where(auto, 0.0, fim * spread)
    fringe = jnp.stack([fre, fim], axis=2).reshape(row_count, col_count, 2, WR * WD)
    weights = baseline_weights(fre, fim)
    col_width = 2 * inputs // chan_devs
    normal_part, rhs_part = normal_terms(weights, row_inputs, col_inputs, inputs)
    arranged = jnp.transpose(normal_part.reshape(2, inputs, 2 * inputs), (1, 0, 2))
    arranged = arranged.reshape(time_devs, row_count, 2, chan_devs, col_width)
    arranged = jnp.transpose(arranged, (0, 3, 1, 2, 4)).reshape(
        time_devs * chan_devs * row_count, 2, col_width
    )
    normal_rows = lax.psum_scatter(arranged, ("tm", "chan"), scatter_dimension=0, tiled=True)
    rhs_all = lax.psum(jnp.transpose(rhs_part.reshape(2, inputs), (1, 0)), ("tm", "chan"))
    rhs_rows = lax.dynamic_slice_in_dim(rhs_all, lax.axis_index("tm") * row_count, row_count, 0)
    columns = lax.axis_index("chan") * col_width + jnp.arange(col_width, dtype=jnp.int32)
    params = jnp.arange(2, dtype=jnp.int32)[None, :] * inputs + row_inputs[:, None]
    row_ref = row_inputs // 2 == ref_station[0]
    col_ref = columns % inputs // 2 == ref_station[0]
    ident = (params[:, :, None] == columns[None, None, :]).astype(jnp.float32)
    normal_rows = jnp.where(row_ref[:, None, None] | col_ref[None, None, :], ident, normal_rows)
    rhs_rows = jnp.where(row_ref[:, None], 0.0, rhs_rows)
    return (fringe, normal_rows, rhs_rows)


TM = 8
MESH = pl.DeviceIdType.MESH
TURN = 2 * BAND


def unit(steps):
    quarter = TURN // 4
    quad = lax.shift_right_logical(steps + quarter // 2, quarter.bit_length() - 1)
    x = (steps - quad * quarter).astype(jnp.float32) * (2.0 * math.pi / TURN)
    y = x * x
    s = x * (1.0 + y * (-1.0 / 6 + y * (1.0 / 120 + y * (-1.0 / 5040 + y * (1.0 / 362880)))))
    c = 1.0 + y * (-0.5 + y * (1.0 / 24 + y * (-1.0 / 720 + y * (1.0 / 40320 + y * (-1.0 / 3628800)))))
    odd = (quad & 1) == 1
    cosine = jnp.where(odd, s, c)
    sine = jnp.where(odd, c, s)
    cosine = jnp.where(((quad + 1) & 2) == 2, -cosine, cosine)
    sine = jnp.where((quad & 2) == 2, -sine, sine)
    return cosine, sine


def cmul(a, b):
    return a[0] * b[0] - a[1] * b[1], a[0] * b[1] + a[1] * b[0]


def cadd(a, b):
    return b if a is None else (a[0] + b[0], a[1] + b[1])


def cconst(a, turns):
    turns = turns % 1.0
    if turns == 0.0:
        return a
    if turns == 0.25:
        return a[1], -a[0]
    if turns == 0.5:
        return -a[0], -a[1]
    if turns == 0.75:
        return -a[1], a[0]
    c, s = math.cos(2 * math.pi * turns), math.sin(2 * math.pi * turns)
    return a[0] * c + a[1] * s, a[1] * c - a[0] * s


def fused(
    nchan, volts, dpk, rpk, order_in, ref, fringe_out, normal_out, rhs_out,
    xbuf, dbuf, rbuf, order, vis, rv, pkl, pka, pnat, sbuf, rb2, zs, rz, wz, nat, rx,
    vsem, isem, bsend, brecv, s1, r1, s2, r2, s3, r3, s4, r4, s5, r5,
):
    i, j = lax.axis_index("tm"), lax.axis_index("chan")
    periods, chans, samples, width = volts.shape
    inputs = width // 2
    rows, cols = dpk.shape
    chans_total = chans * nchan
    core, cx, cy = i % 2, (i // 2) % 2, i // 4
    sibling = i + 1 - 2 * core
    scale = float(samples * TM) ** (-0.5) * float(periods * chans_total) ** (-0.5)

    def chip(r, c):
        return ((((cy + r // 2) % 2) * 2) + (cx + r % 2) % 2) * 2 + c

    def load(n):
        return pltpu.make_async_copy(volts.at[n // chans, n % chans], xbuf.at[n], vsem.at[n])

    def remote(src, dst, ssem, rsem, to_i, to_j):
        return pltpu.make_async_remote_copy(
            src_ref=src, dst_ref=dst, send_sem=ssem, recv_sem=rsem,
            device_id=(to_i, to_j), device_id_type=MESH,
        )

    @pl.loop(0, periods * chans)
    def _(n):
        load(n).start()

    small = [
        pltpu.make_async_copy(src, dst, isem.at[n])
        for n, (src, dst) in enumerate([(dpk, dbuf), (rpk, rbuf), (order_in, order)])
    ]
    for copy in small:
        copy.start()

    barrier = pltpu.get_barrier_semaphore()
    mates = [(r, d) for r in range(4) for d in range(nchan) if r or d]
    for r, d in mates:
        pl.semaphore_signal(
            barrier, inc=1, device_id=(chip(r, core), (j + d) % nchan), device_id_type=MESH
        )
    for r in range(4):
        pl.semaphore_signal(barrier, inc=1, device_id=(chip(r, 1 - core), j), device_id_type=MESH)

    for copy in small:
        copy.wait()
    half = rows // 2
    for h in range(2):
        at = slice(h * half, h * half + half)
        pkl[:, 2 * h * cols : (2 * h + 1) * cols] = dbuf[at, :]
        pkl[:, (2 * h + 1) * cols : (2 * h + 2) * cols] = rbuf[at, :]
    home = cy * 2 + cx
    pka[home, j] = pkl[...]

    def gram(n):
        load(n).wait()
        x = xbuf[n]
        g = lax.dot_general(x, x, (((0,), (0,)), ((), ())), preferred_element_type=jnp.float32)
        re = g[:inputs, :inputs] + g[inputs:, inputs:]
        im = g[:inputs, inputs:] - g[inputs:, :inputs]
        for c in range(2):
            for p in range(4):
                at = slice((2 * p + c) * rows, (2 * p + c + 1) * rows)
                vis[c, n, 0, p * rows : (p + 1) * rows, :] = re[at]
                vis[c, n, 1, p * rows : (p + 1) * rows, :] = im[at]

    def swap(n):
        return remote(vis.at[1 - core, n], rv.at[n], s1.at[n], r1.at[n], sibling, j)

    steps = periods * chans
    early = 6

    @pl.loop(0, early)
    def _(n):
        gram(n)

    hot = (
        lax.broadcasted_iota(jnp.int32, (inputs, inputs), 0)
        == jnp.broadcast_to(order[...], (inputs, inputs))
    ).astype(jnp.float32)
    hot_t = hot.T

    pl.semaphore_wait(barrier, len(mates) + 4)
    bcopies = [
        remote(pkl, pka.at[home, j], bsend.at[e], brecv.at[e], chip(r, core), (j + d) % nchan)
        for e, (r, d) in enumerate(mates)
    ]
    for copy in bcopies:
        copy.start()

    @pl.loop(0, early)
    def _(n):
        swap(n).start()

    @pl.loop(early, steps)
    def _(n):
        gram(n)
        swap(n).start()

    for copy in bcopies:
        copy.wait()

    def gathered(k):
        return jnp.concatenate(
            [
                jnp.concatenate(
                    [
                        pka[c, g][:, (2 * h + k) * cols : (2 * h + k + 1) * cols]
                        for g in range(nchan)
                    ],
                    axis=1,
                )
                for c in range(4)
                for h in range(2)
            ],
            axis=0,
        )

    dall, rall = gathered(0), gathered(1)
    digits = jnp.concatenate(
        [
            lax.shift_right_logical(dall, 8).astype(jnp.float32),
            (dall & 255).astype(jnp.float32),
            rall.astype(jnp.float32),
        ],
        axis=0,
    )
    moved = jnp.dot(
        digits.astype(jnp.bfloat16), hot_t.astype(jnp.bfloat16), preferred_element_type=jnp.float32
    )
    own = 4 * rows
    pnat[0] = (moved[0:own] * 256.0 + moved[own : 2 * own]).astype(jnp.int32)
    pnat[1] = moved[2 * own : 3 * own].astype(jnp.int32)

    @pl.loop(0, steps)
    def _(n):
        swap(n).wait()

    def by_chan(values):
        pick = jnp.float32(values[0])
        for g in range(1, nchan):
            pick = jnp.where(j == g, jnp.float32(values[g]), pick)
        return pick

    dturn = (BAND // chans_total) / TURN
    rturn = (PERIODS_ALL // periods) / (2 * PERIODS_ALL)
    shifts = []
    for wd in range(WD):
        angles = [2 * math.pi * (wd - WD // 2) * g * chans * dturn for g in range(nchan)]
        shifts.append(
            (by_chan([math.cos(t) for t in angles]), by_chan([-math.sin(t) for t in angles]))
        )

    def window(cc, h):
        at = pl.ds(pl.multiple_of(cc * rows + h * 8, 8), 8)
        dl = pnat[0, at, :]
        rl = pnat[1, at, :]
        c, s = unit(dl)
        z1 = (c, -s)
        c, s = unit((dl * (j * chans)) & (TURN - 1))
        ed = (c, -s)
        c, s = unit(rl * (BAND // PERIODS_ALL))
        er = [None, (c, -s)]
        for a in range(2, periods):
            er.append(cmul(er[-1], er[1]))
        acc = [None] * (WR * WD)
        for l in range(chans):
            us = [None] * WR
            for a in range(periods):
                n = a * chans + l
                v = (
                    vis[core, n, 0, at, :] + rv[n, 0, at, :],
                    vis[core, n, 1, at, :] + rv[n, 1, at, :],
                )
                if a:
                    v = cmul(v, er[a])
                for wr in range(WR):
                    us[wr] = cadd(us[wr], cconst(v, (wr - WR // 2) * a * rturn))
            if l:
                ed = cmul(ed, z1)
            for wr in range(WR):
                u = cmul(us[wr], ed)
                for wd in range(WD):
                    term = cconst(u, (wd - WD // 2) * l * dturn)
                    acc[wr * WD + wd] = cadd(acc[wr * WD + wd], term)
        out = []
        for w in range(WR * WD):
            wd = w % WD
            out.append(acc[w] if wd == WD // 2 else cmul(acc[w], shifts[wd]))
        return [o[0] for o in out] + [o[1] for o in out]

    @pl.loop(0, 4)
    def _(u):
        r = 3 - u
        for h in range(rows // 8):
            values = window(chip(r, core) // 2, h)
            for v, value in enumerate(values):
                sbuf[r, v, h * 8 : h * 8 + 8, :] = value

        @pl.when(r > 0)
        def _():
            remote(sbuf.at[r], rb2.at[r - 1], s2.at[r - 1], r2.at[r - 1], chip(r, core), j).start()

    bins = WR * WD
    row = lax.broadcasted_iota(jnp.int32, (bins * rows, inputs), 0)
    col = lax.broadcasted_iota(jnp.int32, (bins * rows, inputs), 1)
    w_row, kind = row // rows, col // rows
    ud = (2 * (w_row % WD) + 1 - WD).astype(jnp.float32) / WD
    ur = (2 * (w_row // WD) + 1 - WR).astype(jnp.float32) / WR
    coef = jnp.where(kind == 0, ud * ud, 0.0)
    coef = jnp.where(kind == 1, ud * ur, coef)
    coef = jnp.where(kind == 2, ur * ur, coef)
    coef = jnp.where(kind == 3, ud, coef)
    coef = jnp.where(kind == 4, ur, coef)
    coef = jnp.where(row % rows == col % rows, coef, 0.0) * (1.0 / bins)

    for r in (1, 2, 3):
        remote(sbuf.at[r], rb2.at[r - 1], s2.at[r - 1], r2.at[r - 1], chip(r, core), j).wait()
    total = (sbuf[0] + rb2[0]) + (rb2[1] + rb2[2])
    shape3 = (2 * bins, rows, inputs)
    auto = lax.broadcasted_iota(jnp.int32, shape3, 2) == (
        lax.broadcasted_iota(jnp.int32, shape3, 1) + i * rows
    )
    total = jnp.where(auto, 0.0, total * scale).reshape(2 * bins * rows, inputs)
    zs[...] = lax.dot_general(
        hot_t, total, (((1,), (1,)), ((), ())),
        precision=lax.Precision.HIGHEST, preferred_element_type=jnp.float32,
    )

    def group(g):
        return pl.ds(pl.multiple_of(g * cols, cols), cols)

    copies = []
    for d in range(1, nchan):
        to = (j + d) % nchan
        copies.append(remote(zs.at[group(to)], rz.at[d - 1], s3.at[d - 1], r3.at[d - 1], i, to))
        copies[-1].start()
    mine = zs[group(j), :]
    for d, copy in enumerate(copies):
        copy.wait()
        mine = mine + rz[d]
    fre, fim = mine[:, : bins * rows], mine[:, bins * rows :]
    power = fre * fre + fim * fim
    wz[group(j), :] = jnp.dot(
        power, coef, precision=lax.Precision.HIGHEST, preferred_element_type=jnp.float32
    )
    copies = []
    for d in range(1, nchan):
        to = (j + d) % nchan
        copies.append(remote(wz.at[group(j)], wz.at[group(j)], s4.at[d - 1], r4.at[d - 1], i, to))
        copies[-1].start()
    turned = mine.T.reshape(2 * bins, rows, cols)
    fringe_out[...] = jnp.swapaxes(turned, 0, 1)
    for copy in copies:
        copy.wait()
    natural = jnp.dot(
        hot, wz[...], precision=lax.Precision.HIGHEST, preferred_element_type=jnp.float32
    )
    nat[...] = natural

    def rowsof(g):
        return pl.ds(pl.multiple_of(g * rows, rows), rows)

    copies = []
    for d in range(1, TM):
        to = (i + d) % TM
        copies.append(remote(nat.at[rowsof(to)], rx.at[i], s5.at[d - 1], r5.at[d - 1], to, j))
        copies[-1].start()
    rx[i] = nat[rowsof(i), :]
    straight = natural.T
    for copy in copies:
        copy.wait()
    across = [
        jnp.concatenate([rx[g, :, m * rows : (m + 1) * rows] for g in range(TM)], axis=1)
        for m in range(5)
    ]
    straight = [straight[m * rows : (m + 1) * rows] for m in range(5)]
    row_in = lax.broadcasted_iota(jnp.int32, (rows, inputs), 0) + i * rows
    col_in = lax.broadcasted_iota(jnp.int32, (rows, inputs), 1)
    diag = row_in == col_in
    isref = (lax.shift_right_logical(row_in, 1) == ref[0]) | (
        lax.shift_right_logical(col_in, 1) == ref[0]
    )
    blocks = []
    for m in range(3):
        both = straight[m] + across[m]
        sums = jnp.sum(both, axis=1, keepdims=True)
        blocks.append((jnp.where(diag, sums, 0.0) - both) * (1.0 / inputs))
    t = j * 2 // nchan
    per = nchan // 2
    span = 2 * inputs // nchan
    for s in range(2):
        block = jnp.where(t == 0, blocks[s], blocks[s + 1])
        ident = jnp.where(diag & (t == s), 1.0, 0.0)
        block = jnp.where(isref, ident, block)
        out = block[:, 0:span]
        for q in range(1, per):
            out = jnp.where(j % per == q, block[:, q * span : (q + 1) * span], out)
        normal_out[:, s, :] = out
    lane = lax.broadcasted_iota(jnp.int32, (rows, inputs), 1)
    right = jnp.zeros((rows, inputs), jnp.float32)
    for s in range(2):
        value = jnp.sum(straight[3 + s] - across[3 + s], axis=1, keepdims=True) * (1.0 / inputs)
        right = jnp.where(lane == s, value, right)
    right = jnp.where(lax.shift_right_logical(row_in, 1) == ref[0], 0.0, right)
    rhs_out[...] = right.T[0:2, :]


def emit(*refs):
    for src, dst in zip(refs[:3], refs[3:]):
        dst[...] = src[...]


def fused_body(nchan, volts, delay_peak, rate_peak, station_order, ref_station):
    periods, chans, samples, width = volts.shape
    inputs = width // 2
    rows, cols = delay_peak.shape
    bins = WR * WD
    steps = periods * chans
    f32 = jnp.float32
    vmem = pl.BlockSpec(memory_space=pltpu.VMEM)
    dma = pltpu.SemaphoreType.DMA
    out_shape = (
        jax.ShapeDtypeStruct((rows, 2 * bins, cols), f32),
        jax.ShapeDtypeStruct((rows, 2, 2 * inputs // nchan), f32),
        jax.ShapeDtypeStruct((2, rows), f32),
    )
    hbm = pl.BlockSpec(memory_space=pltpu.HBM)
    results = pl.pallas_call(
        functools.partial(fused, nchan),
        out_shape=out_shape,
        in_specs=[hbm, hbm, hbm, hbm, pl.BlockSpec(memory_space=pltpu.SMEM)],
        out_specs=(vmem, vmem, vmem),
        scratch_shapes=[
            pltpu.VMEM((steps, samples, width), volts.dtype),
            pltpu.VMEM((rows, cols), jnp.int32),
            pltpu.VMEM((rows, cols), jnp.int32),
            pltpu.VMEM((1, inputs), jnp.int32),
            pltpu.VMEM((2, steps, 2, 4 * rows, inputs), f32),
            pltpu.VMEM((steps, 2, 4 * rows, inputs), f32),
            pltpu.VMEM((rows // 2, 4 * cols), jnp.int32),
            pltpu.VMEM((4, nchan, rows // 2, 4 * cols), jnp.int32),
            pltpu.VMEM((2, 4 * rows, inputs), jnp.int32),
            pltpu.VMEM((4, 2 * bins, rows, inputs), f32),
            pltpu.VMEM((3, 2 * bins, rows, inputs), f32),
            pltpu.VMEM((inputs, 2 * bins * rows), f32),
            pltpu.VMEM((nchan - 1, cols, 2 * bins * rows), f32),
            pltpu.VMEM((inputs, inputs), f32),
            pltpu.VMEM((inputs, inputs), f32),
            pltpu.VMEM((TM, rows, inputs), f32),
            dma((steps,)), dma((3,)),
            dma((4 * nchan - 1,)), dma((4 * nchan - 1,)),
            dma((steps,)), dma((steps,)),
            dma((3,)), dma((3,)),
            dma((nchan - 1,)), dma((nchan - 1,)),
            dma((nchan - 1,)), dma((nchan - 1,)),
            dma((TM - 1,)), dma((TM - 1,)),
        ],
        compiler_params=pltpu.CompilerParams(
            collective_id=0, has_side_effects=True, vmem_limit_bytes=48 * 1024 * 1024
        ),
        name="fringe_fit",
    )(volts, delay_peak, rate_peak, station_order.reshape(1, inputs), ref_station)
    fringe, normal, rhs = pl.pallas_call(
        emit, out_shape=out_shape, in_specs=[vmem] * 3, out_specs=(vmem,) * 3, name="emit",
        compiler_params=pltpu.CompilerParams(vmem_limit_bytes=4 * 1024 * 1024),
    )(*results)
    fringe = jnp.transpose(fringe.reshape(rows, 2, bins, cols), (0, 3, 1, 2))
    return fringe, normal, jnp.transpose(rhs)


def solution(mesh):
    in_specs = (P(None, "chan", "tm", None), P("tm", "chan"), P("tm", "chan"), P(), P())
    out_specs = (P("tm", "chan", None, None), P("tm", None, "chan"), P("tm", None))
    nchan = mesh.shape["chan"]
    fits = mesh.shape["tm"] == TM and nchan == 4
    whole = functools.partial(fused_body, nchan) if fits else body
    return jax.shard_map(whole, mesh=mesh, in_specs=in_specs, out_specs=out_specs, check_vma=False)
```

```python
import functools
import math

import jax
import jax.numpy as jnp
from jax import lax
from jax.experimental import pallas as pl
from jax.experimental.pallas import tpu as pltpu
from jax.sharding import PartitionSpec as P

BAND = 16384
PERIODS_ALL = 8
WD = 4
WR = 2


def fringe_window(vis_re, vis_im, dpeak, rpeak, chans_total, periods):
    chan_local = vis_re.shape[3]
    dgrid = 2 * BAND
    rgrid = 2 * PERIODS_ALL
    dstep = BAND // chans_total
    rstep = PERIODS_ALL // periods
    chan_idx = jnp.arange(chan_local, dtype=jnp.int32)
    period_idx = jnp.arange(periods, dtype=jnp.int32)
    delays = dpeak[:, :, None] + (jnp.arange(WD, dtype=jnp.int32) - WD // 2) * dstep
    rates = rpeak[:, :, None] + (jnp.arange(WR, dtype=jnp.int32) - WR // 2) * rstep
    dphase = jnp.mod(delays[..., None] * chan_idx, dgrid).astype(jnp.float32) * (
        2.0 * math.pi / dgrid
    )
    rphase = jnp.mod(rates[..., None] * period_idx, rgrid).astype(jnp.float32) * (
        2.0 * math.pi / rgrid
    )
    angle = rphase[:, :, :, None, :, None] + dphase[:, :, None, :, None, :]
    cosine = jnp.cos(angle)
    sine = jnp.sin(angle)
    vr = vis_re[:, :, None, None]
    vi = vis_im[:, :, None, None]
    fre = jnp.sum(vr * cosine + vi * sine, axis=(4, 5))
    fim = jnp.sum(vi * cosine - vr * sine, axis=(4, 5))
    return (fre, fim)


def baseline_weights(fre, fim):
    power = fre * fre + fim * fim
    udel = (2.0 * jnp.arange(WD, dtype=jnp.float32) + 1.0 - WD) / WD
    urat = (2.0 * jnp.arange(WR, dtype=jnp.float32) + 1.0 - WR) / WR
    udel = udel[None, :]
    urat = urat[:, None]
    m_dd = jnp.mean(power * udel * udel, axis=(2, 3))
    m_dr = jnp.mean(power * udel * urat, axis=(2, 3))
    m_rr = jnp.mean(power * urat * urat, axis=(2, 3))
    g_d = jnp.mean(power * udel, axis=(2, 3))
    g_r = jnp.mean(power * urat, axis=(2, 3))
    return jnp.stack([m_dd, m_dr, m_rr, g_d, g_r])


def normal_terms(weights, row_inputs, col_inputs, inputs):
    slots = jnp.arange(inputs, dtype=jnp.int32)
    incidence = (row_inputs[:, None, None] == slots).astype(jnp.float32) - (
        col_inputs[None, :, None] == slots
    ).astype(jnp.float32)
    flat = incidence.reshape(-1, inputs)

    def block(weight):
        scaled = (incidence * weight[:, :, None]).reshape(-1, inputs)
        return jnp.dot(scaled.T, flat, precision=lax.Precision.HIGHEST) / inputs

    n_dd = block(weights[0])
    n_dr = block(weights[1])
    n_rr = block(weights[2])
    normal = jnp.concatenate(
        [jnp.concatenate([n_dd, n_dr], 1), jnp.concatenate([n_dr, n_rr], 1)], 0
    )
    rhs_d = jnp.dot(weights[3].reshape(-1), flat, precision=lax.Precision.HIGHEST) / inputs
    rhs_r = jnp.dot(weights[4].reshape(-1), flat, precision=lax.Precision.HIGHEST) / inputs
    return (normal, jnp.concatenate([rhs_d, rhs_r]))


def full_gram(volts, inputs, scale):
    prod = jnp.einsum("acti,actj->iacj", volts, volts, preferred_element_type=jnp.float32)
    real = prod[:inputs, :, :, :inputs] + prod[inputs:, :, :, inputs:]
    imag = prod[:inputs, :, :, inputs:] - prod[inputs:, :, :, :inputs]
    return jnp.stack([real, imag], axis=3) * scale


def body(volts, delay_peak, rate_peak, station_order, ref_station):
    periods, chans, samples, width = volts.shape
    inputs = width // 2
    row_count = delay_peak.shape[0]
    col_count = delay_peak.shape[1]
    time_devs = lax.axis_size("tm")
    chan_devs = lax.axis_size("chan")
    chans_total = chans * chan_devs
    scale = float(samples * time_devs) ** (-0.5)
    spread = float(periods * chans_total) ** (-0.5)
    col_inputs = lax.dynamic_slice_in_dim(
        station_order, lax.axis_index("chan") * col_count, col_count
    )
    row_inputs = lax.axis_index("tm") * row_count + jnp.arange(row_count, dtype=jnp.int32)
    gram = full_gram(volts, inputs, scale)
    summed = lax.psum_scatter(
        gram.reshape(lax.axis_size("tm") * row_count, -1), "tm", scatter_dimension=0, tiled=True
    )
    vis = summed.reshape(row_count, periods, chans, 2, inputs)
    grouped = jnp.take(vis, station_order, axis=4)
    moved = lax.all_to_all(grouped, "chan", split_axis=4, concat_axis=2, tiled=True)
    vis_re = jnp.transpose(moved[:, :, :, 0], (0, 3, 1, 2))
    vis_im = jnp.transpose(moved[:, :, :, 1], (0, 3, 1, 2))
    fre, fim = fringe_window(vis_re, vis_im, delay_peak, rate_peak, chans_total, periods)
    auto = (row_inputs[:, None] == col_inputs[None, :])[:, :, None, None]
    fre = jnp.where(auto, 0.0, fre * spread)
    fim = jnp.where(auto, 0.0, fim * spread)
    fringe = jnp.stack([fre, fim], axis=2).reshape(row_count, col_count, 2, WR * WD)
    weights = baseline_weights(fre, fim)
    col_width = 2 * inputs // chan_devs
    normal_part, rhs_part = normal_terms(weights, row_inputs, col_inputs, inputs)
    arranged = jnp.transpose(normal_part.reshape(2, inputs, 2 * inputs), (1, 0, 2))
    arranged = arranged.reshape(time_devs, row_count, 2, chan_devs, col_width)
    arranged = jnp.transpose(arranged, (0, 3, 1, 2, 4)).reshape(
        time_devs * chan_devs * row_count, 2, col_width
    )
    normal_rows = lax.psum_scatter(arranged, ("tm", "chan"), scatter_dimension=0, tiled=True)
    rhs_all = lax.psum(jnp.transpose(rhs_part.reshape(2, inputs), (1, 0)), ("tm", "chan"))
    rhs_rows = lax.dynamic_slice_in_dim(rhs_all, lax.axis_index("tm") * row_count, row_count, 0)
    columns = lax.axis_index("chan") * col_width + jnp.arange(col_width, dtype=jnp.int32)
    params = jnp.arange(2, dtype=jnp.int32)[None, :] * inputs + row_inputs[:, None]
    row_ref = row_inputs // 2 == ref_station[0]
    col_ref = columns % inputs // 2 == ref_station[0]
    ident = (params[:, :, None] == columns[None, None, :]).astype(jnp.float32)
    normal_rows = jnp.where(row_ref[:, None, None] | col_ref[None, None, :], ident, normal_rows)
    rhs_rows = jnp.where(row_ref[:, None], 0.0, rhs_rows)
    return (fringe, normal_rows, rhs_rows)


TM = 8
MESH = pl.DeviceIdType.MESH
TURN = 2 * BAND


def unit(steps):
    quarter = TURN // 4
    quad = lax.shift_right_logical(steps + quarter // 2, quarter.bit_length() - 1)
    x = (steps - quad * quarter).astype(jnp.float32) * (2.0 * math.pi / TURN)
    y = x * x
    s = x * (1.0 + y * (-1.0 / 6 + y * (1.0 / 120 + y * (-1.0 / 5040 + y * (1.0 / 362880)))))
    c = 1.0 + y * (-0.5 + y * (1.0 / 24 + y * (-1.0 / 720 + y * (1.0 / 40320 + y * (-1.0 / 3628800)))))
    odd = (quad & 1) == 1
    cosine = jnp.where(odd, s, c)
    sine = jnp.where(odd, c, s)
    cosine = jnp.where(((quad + 1) & 2) == 2, -cosine, cosine)
    sine = jnp.where((quad & 2) == 2, -sine, sine)
    return cosine, sine


def cmul(a, b):
    return a[0] * b[0] - a[1] * b[1], a[0] * b[1] + a[1] * b[0]


def cadd(a, b):
    return b if a is None else (a[0] + b[0], a[1] + b[1])


def cconst(a, turns):
    turns = turns % 1.0
    if turns == 0.0:
        return a
    if turns == 0.25:
        return a[1], -a[0]
    if turns == 0.5:
        return -a[0], -a[1]
    if turns == 0.75:
        return -a[1], a[0]
    c, s = math.cos(2 * math.pi * turns), math.sin(2 * math.pi * turns)
    return a[0] * c + a[1] * s, a[1] * c - a[0] * s


def fused(
    nchan, rows, cols, volts, packed, ref, fringe_out, normal_out, rhs_out,
    xbuf, vis, rv, pkl, pka, pnat, sbuf, rb2, zs, rz, wz, nat, rx,
    vsem, bsend, brecv, s1, r1, s2, r2, s3, r3, s4, r4, s5, r5,
):
    i, j = lax.axis_index("tm"), lax.axis_index("chan")
    periods, chans, samples, width = volts.shape
    inputs = width // 2
    chans_total = chans * nchan
    core, cx, cy = i % 2, (i // 2) % 2, i // 4
    sibling = i + 1 - 2 * core
    scale = float(samples * TM) ** (-0.5) * float(periods * chans_total) ** (-0.5)

    def chip(r, c):
        return ((((cy + r // 2) % 2) * 2) + (cx + r % 2) % 2) * 2 + c

    def load(n):
        return pltpu.make_async_copy(volts.at[n // chans, n % chans], xbuf.at[n], vsem.at[n])

    def remote(src, dst, ssem, rsem, to_i, to_j):
        return pltpu.make_async_remote_copy(
            src_ref=src, dst_ref=dst, send_sem=ssem, recv_sem=rsem,
            device_id=(to_i, to_j), device_id_type=MESH,
        )

    @pl.loop(0, periods * chans)
    def _(n):
        load(n).start()

    barrier = pltpu.get_barrier_semaphore()
    mates = [(r, d) for r in range(4) for d in range(nchan) if r or d]
    for r, d in mates:
        pl.semaphore_signal(
            barrier, inc=1, device_id=(chip(r, core), (j + d) % nchan), device_id_type=MESH
        )
    for r in range(4):
        pl.semaphore_signal(barrier, inc=1, device_id=(chip(r, 1 - core), j), device_id_type=MESH)

    half = rows // 2
    pkl[...] = packed[0:half, :]
    home = cy * 2 + cx
    pka[home, j] = pkl[...]

    def gram(n):
        load(n).wait()
        x = xbuf[n]
        g = lax.dot_general(x, x, (((0,), (0,)), ((), ())), preferred_element_type=jnp.float32)
        re = g[:inputs, :inputs] + g[inputs:, inputs:]
        im = g[:inputs, inputs:] - g[inputs:, :inputs]
        for c in range(2):
            for p in range(4):
                at = slice((2 * p + c) * rows, (2 * p + c + 1) * rows)
                vis[c, n, 0, p * rows : (p + 1) * rows, :] = re[at]
                vis[c, n, 1, p * rows : (p + 1) * rows, :] = im[at]

    def swap(n):
        return remote(vis.at[1 - core, n], rv.at[n], s1.at[n], r1.at[n], sibling, j)

    steps = periods * chans
    early = 6

    @pl.loop(0, early)
    def _(n):
        gram(n)

    hot = (
        lax.broadcasted_iota(jnp.int32, (inputs, inputs), 0)
        == jnp.broadcast_to(packed[half : half + 1, :], (inputs, inputs))
    ).astype(jnp.float32)
    hot_t = hot.T

    pl.semaphore_wait(barrier, len(mates) + 4)
    bcopies = [
        remote(pkl, pka.at[home, j], bsend.at[e], brecv.at[e], chip(r, core), (j + d) % nchan)
        for e, (r, d) in enumerate(mates)
    ]
    for copy in bcopies:
        copy.start()

    @pl.loop(0, early)
    def _(n):
        swap(n).start()

    @pl.loop(early, steps)
    def _(n):
        gram(n)
        swap(n).start()

    for copy in bcopies:
        copy.wait()

    def gathered(k):
        return jnp.concatenate(
            [
                jnp.concatenate(
                    [
                        pka[c, g][:, (2 * h + k) * cols : (2 * h + k + 1) * cols]
                        for g in range(nchan)
                    ],
                    axis=1,
                )
                for c in range(4)
                for h in range(2)
            ],
            axis=0,
        )

    dall, rall = gathered(0), gathered(1)
    digits = jnp.concatenate(
        [
            lax.shift_right_logical(dall, 8).astype(jnp.float32),
            (dall & 255).astype(jnp.float32),
            rall.astype(jnp.float32),
        ],
        axis=0,
    )
    moved = jnp.dot(
        digits.astype(jnp.bfloat16), hot_t.astype(jnp.bfloat16), preferred_element_type=jnp.float32
    )
    own = 4 * rows
    pnat[0] = (moved[0:own] * 256.0 + moved[own : 2 * own]).astype(jnp.int32)
    pnat[1] = moved[2 * own : 3 * own].astype(jnp.int32)

    @pl.loop(0, steps)
    def _(n):
        swap(n).wait()

    def by_chan(values):
        pick = jnp.float32(values[0])
        for g in range(1, nchan):
            pick = jnp.where(j == g, jnp.float32(values[g]), pick)
        return pick

    dturn = (BAND // chans_total) / TURN
    rturn = (PERIODS_ALL // periods) / (2 * PERIODS_ALL)
    shifts = []
    for wd in range(WD):
        angles = [2 * math.pi * (wd - WD // 2) * g * chans * dturn for g in range(nchan)]
        shifts.append(
            (by_chan([math.cos(t) for t in angles]), by_chan([-math.sin(t) for t in angles]))
        )

    def window(cc, h):
        at = pl.ds(pl.multiple_of(cc * rows + h * 8, 8), 8)
        dl = pnat[0, at, :]
        rl = pnat[1, at, :]
        c, s = unit(dl)
        z1 = (c, -s)
        c, s = unit((dl * (j * chans)) & (TURN - 1))
        ed = (c, -s)
        c, s = unit(rl * (BAND // PERIODS_ALL))
        er = [None, (c, -s)]
        for a in range(2, periods):
            er.append(cmul(er[-1], er[1]))
        acc = [None] * (WR * WD)
        for l in range(chans):
            us = [None] * WR
            for a in range(periods):
                n = a * chans + l
                v = (
                    vis[core, n, 0, at, :] + rv[n, 0, at, :],
                    vis[core, n, 1, at, :] + rv[n, 1, at, :],
                )
                if a:
                    v = cmul(v, er[a])
                for wr in range(WR):
                    us[wr] = cadd(us[wr], cconst(v, (wr - WR // 2) * a * rturn))
            if l:
                ed = cmul(ed, z1)
            for wr in range(WR):
                u = cmul(us[wr], ed)
                for wd in range(WD):
                    term = cconst(u, (wd - WD // 2) * l * dturn)
                    acc[wr * WD + wd] = cadd(acc[wr * WD + wd], term)
        out = []
        for w in range(WR * WD):
            wd = w % WD
            out.append(acc[w] if wd == WD // 2 else cmul(acc[w], shifts[wd]))
        return [o[0] for o in out] + [o[1] for o in out]

    def plane(h, r):
        return remote(
            sbuf.at[h, r], rb2.at[h, r - 1], s2.at[h, r - 1], r2.at[h, r - 1], chip(r, core), j
        )

    @pl.loop(0, 8)
    def _(u):
        h, r = u // 4, 3 - u % 4
        for v, value in enumerate(window(chip(r, core) // 2, h)):
            sbuf[h, r, v] = value

        @pl.when(r > 0)
        def _():
            plane(h, r).start()

    bins = WR * WD
    tall = 2 * bins * rows
    row = lax.broadcasted_iota(jnp.int32, (tall, inputs), 0)
    col = lax.broadcasted_iota(jnp.int32, (tall, inputs), 1)
    p_row = row // (2 * bins * half) * half + row % half
    w_row, kind = row // half % bins, col // rows
    ud = (2 * (w_row % WD) + 1 - WD).astype(jnp.float32) / WD
    ur = (2 * (w_row // WD) + 1 - WR).astype(jnp.float32) / WR
    coef = jnp.where(kind == 0, ud * ud, 0.0)
    coef = jnp.where(kind == 1, ud * ur, coef)
    coef = jnp.where(kind == 2, ur * ur, coef)
    coef = jnp.where(kind == 3, ud, coef)
    coef = jnp.where(kind == 4, ur, coef)
    coef = jnp.where(p_row == col % rows, coef, 0.0) * (1.0 / bins)

    def group(g):
        return pl.ds(pl.multiple_of(g * cols, cols), cols)

    shape3 = (2 * bins, half, inputs)
    lane3 = lax.broadcasted_iota(jnp.int32, shape3, 2)
    row3 = lax.broadcasted_iota(jnp.int32, shape3, 1) + i * rows
    zcopies = []
    for h in range(2):
        for r in (3, 2, 1):
            plane(h, r).wait()
        total = (sbuf[h, 0] + rb2[h, 0]) + (rb2[h, 1] + rb2[h, 2])
        total = jnp.where(lane3 == row3 + h * half, 0.0, total * scale)
        zs[h] = lax.dot_general(
            hot_t, total.reshape(2 * bins * half, inputs), (((1,), (1,)), ((), ())),
            precision=lax.Precision.HIGHEST, preferred_element_type=jnp.float32,
        )
        for d in range(1, nchan):
            to = (j + d) % nchan
            zcopies.append(
                remote(zs.at[h, group(to)], rz.at[h, d - 1], s3.at[h, d - 1], r3.at[h, d - 1], i, to)
            )
            zcopies[-1].start()
    parts = []
    for h in range(2):
        mine = zs[h, group(j), :]
        for d in range(1, nchan):
            zcopies[h * (nchan - 1) + d - 1].wait()
            mine = mine + rz[h, d - 1]
        parts.append(mine)
    mine = jnp.concatenate(parts, axis=1)
    wz[group(j), :] = jnp.dot(
        mine * mine, coef, precision=lax.Precision.HIGHEST, preferred_element_type=jnp.float32
    )
    copies = []
    for d in range(1, nchan):
        to = (j + d) % nchan
        copies.append(remote(wz.at[group(j)], wz.at[group(j)], s4.at[d - 1], r4.at[d - 1], i, to))
        copies[-1].start()
    for h in range(2):
        turned = parts[h].T.reshape(2 * bins, half, cols)
        fringe_out[h * half : (h + 1) * half] = jnp.swapaxes(turned, 0, 1)
    for copy in copies:
        copy.wait()
    natural = jnp.dot(
        hot, wz[...], precision=lax.Precision.HIGHEST, preferred_element_type=jnp.float32
    )
    nat[...] = natural

    def rowsof(g):
        return pl.ds(pl.multiple_of(g * rows, rows), rows)

    copies = []
    for d in range(1, TM):
        to = (i + d) % TM
        copies.append(remote(nat.at[rowsof(to)], rx.at[i], s5.at[d - 1], r5.at[d - 1], to, j))
        copies[-1].start()
    rx[i] = nat[rowsof(i), :]
    straight = natural.T
    for copy in copies:
        copy.wait()
    across = [
        jnp.concatenate([rx[g, :, m * rows : (m + 1) * rows] for g in range(TM)], axis=1)
        for m in range(5)
    ]
    straight = [straight[m * rows : (m + 1) * rows] for m in range(5)]
    row_in = lax.broadcasted_iota(jnp.int32, (rows, inputs), 0) + i * rows
    col_in = lax.broadcasted_iota(jnp.int32, (rows, inputs), 1)
    diag = row_in == col_in
    isref = (lax.shift_right_logical(row_in, 1) == ref[0]) | (
        lax.shift_right_logical(col_in, 1) == ref[0]
    )
    blocks = []
    for m in range(3):
        both = straight[m] + across[m]
        sums = jnp.sum(both, axis=1, keepdims=True)
        blocks.append((jnp.where(diag, sums, 0.0) - both) * (1.0 / inputs))
    t = j * 2 // nchan
    per = nchan // 2
    span = 2 * inputs // nchan
    for s in range(2):
        block = jnp.where(t == 0, blocks[s], blocks[s + 1])
        ident = jnp.where(diag & (t == s), 1.0, 0.0)
        block = jnp.where(isref, ident, block)
        out = block[:, 0:span]
        for q in range(1, per):
            out = jnp.where(j % per == q, block[:, q * span : (q + 1) * span], out)
        normal_out[:, s, :] = out
    lane = lax.broadcasted_iota(jnp.int32, (rows, inputs), 1)
    right = jnp.zeros((rows, inputs), jnp.float32)
    for s in range(2):
        value = jnp.sum(straight[3 + s] - across[3 + s], axis=1, keepdims=True) * (1.0 / inputs)
        right = jnp.where(lane == s, value, right)
    right = jnp.where(lax.shift_right_logical(row_in, 1) == ref[0], 0.0, right)
    rhs_out[...] = right.T[0:2, :]


def emit(*refs):
    for src, dst in zip(refs[:3], refs[3:]):
        dst[...] = src[...]


def fused_body(nchan, volts, delay_peak, rate_peak, station_order, ref_station):
    periods, chans, samples, width = volts.shape
    inputs = width // 2
    rows, cols = delay_peak.shape
    bins = WR * WD
    steps = periods * chans
    f32 = jnp.float32
    vmem = pl.BlockSpec(memory_space=pltpu.VMEM)
    dma = pltpu.SemaphoreType.DMA
    out_shape = (
        jax.ShapeDtypeStruct((rows, 2 * bins, cols), f32),
        jax.ShapeDtypeStruct((rows, 2, 2 * inputs // nchan), f32),
        jax.ShapeDtypeStruct((2, rows), f32),
    )
    half = rows // 2
    packed = jnp.concatenate([delay_peak[:half], rate_peak[:half], delay_peak[half:], rate_peak[half:]], 1)
    packed = jnp.concatenate([packed, jnp.broadcast_to(station_order, (half, inputs))], 0)
    results = pl.pallas_call(
        functools.partial(fused, nchan, rows, cols),
        out_shape=out_shape,
        in_specs=[pl.BlockSpec(memory_space=pl.ANY), vmem, pl.BlockSpec(memory_space=pltpu.SMEM)],
        out_specs=(vmem, vmem, vmem),
        scratch_shapes=[
            pltpu.VMEM((steps, samples, width), volts.dtype),
            pltpu.VMEM((2, steps, 2, 4 * rows, inputs), f32),
            pltpu.VMEM((steps, 2, 4 * rows, inputs), f32),
            pltpu.VMEM((rows // 2, 4 * cols), jnp.int32),
            pltpu.VMEM((4, nchan, rows // 2, 4 * cols), jnp.int32),
            pltpu.VMEM((2, 4 * rows, inputs), jnp.int32),
            pltpu.VMEM((2, 4, 2 * bins, half, inputs), f32),
            pltpu.VMEM((2, 3, 2 * bins, half, inputs), f32),
            pltpu.VMEM((2, inputs, 2 * bins * half), f32),
            pltpu.VMEM((2, nchan - 1, cols, 2 * bins * half), f32),
            pltpu.VMEM((inputs, inputs), f32),
            pltpu.VMEM((inputs, inputs), f32),
            pltpu.VMEM((TM, rows, inputs), f32),
            dma((steps,)),
            dma((4 * nchan - 1,)), dma((4 * nchan - 1,)),
            dma((steps,)), dma((steps,)),
            dma((2, 3)), dma((2, 3)),
            dma((2, nchan - 1)), dma((2, nchan - 1)),
            dma((nchan - 1,)), dma((nchan - 1,)),
            dma((TM - 1,)), dma((TM - 1,)),
        ],
        compiler_params=pltpu.CompilerParams(
            collective_id=0, has_side_effects=True, vmem_limit_bytes=48 * 1024 * 1024
        ),
        name="fringe_fit",
    )(volts, packed, ref_station)
    fringe, normal, rhs = pl.pallas_call(
        emit, out_shape=out_shape, in_specs=[vmem] * 3, out_specs=(vmem,) * 3, name="emit",
        compiler_params=pltpu.CompilerParams(vmem_limit_bytes=4 * 1024 * 1024),
    )(*results)
    fringe = jnp.transpose(fringe.reshape(rows, 2, bins, cols), (0, 3, 1, 2))
    return fringe, normal, jnp.transpose(rhs)


def solution(mesh):
    in_specs = (P(None, "chan", "tm", None), P("tm", "chan"), P("tm", "chan"), P(), P())
    out_specs = (P("tm", "chan", None, None), P("tm", None, "chan"), P("tm", None))
    nchan = mesh.shape["chan"]
    fits = mesh.shape["tm"] == TM and nchan == 4
    whole = functools.partial(fused_body, nchan) if fits else body
    return jax.shard_map(whole, mesh=mesh, in_specs=in_specs, out_specs=out_specs, check_vma=False)
```
